32 devices in a mesh: row: 4 (over z), col: 8 (over y, x, core).
Axes of the slice: x: 2, y: 2, z: 4, core: 2. Of those that a mesh axis runs over, the one named last changes fastest.
Arguments:
- ancestor_pivot: float32 [8, 512, 4, 1024], P(None, 'row', None, 'col'), as said below
- child_pivot: float32 [8, 512, 4, 1024], P(None, 'row', None, 'col'), as said below
- child_panel: float32 [8, 512, 4, 1024], P(None, 'row', None, 'col'), may hold values from -0.09375 to 0.09375
- block_pattern: int32 [32, 32], replicated, may hold values 0 or 1
Outputs:
- child_inverse: float32 [8, 512, 4, 1024], P(None, 'row', None, 'col')
The draws below stay inside these ranges and needn't reach their ends.
Inputs may be any that keep to these rules, and one draw needn't show every extreme that they name: ancestor_pivot is an exactly symmetric 4096 x 4096 matrix. child_pivot is an exactly symmetric 4096 x 4096 matrix.
All inputs are finite; a program needn't handle non-finite values.
Results may differ from the reference program's by a relative error of at most 0.00005.
Values sent between devices are 32-bit elements; how exact they have to be, the bound alone decides.
A program may use at most 128 MiB of HBM per device.

```python
import math
import jax
import jax.numpy as jnp
from jax import lax

W = 4096
BS = 128
ANC = 4096
SNB = 32
ANB = 32
LOC_A = 8
LOC_R = 8
LOC_C = 4
N_ROW = 4
N_COL = 8


def symmetric_pivot(key, order):
    key_noise, key_diag = jax.random.split(key, 2)
    indices = jnp.arange(order)
    diagonal = jnp.exp(jax.random.uniform(key_diag, (order,), jnp.float32, 0.0, math.log(4.0)))
    noise = jax.random.truncated_normal(key_noise, -4.0, 4.0, (order, order), jnp.float32)
    offdiag = 0.3 / math.sqrt(order) * (noise + noise.T)
    filled = diagonal[:, None] * jnp.ones((1, order), jnp.float32)
    matrix = jnp.where(indices[:, None] == indices[None, :], filled, offdiag)
    return matrix.reshape(order // (N_ROW * BS), N_ROW * BS, order // (N_COL * BS), N_COL * BS)


def draw_ancestor_pivot(key, part):
    return symmetric_pivot(jax.random.fold_in(key, 11), ANC)


def draw_child_pivot(key, part):
    return symmetric_pivot(jax.random.fold_in(key, 23), W)


def with_ends(entries, own_key, least, largest):
    index_at = [jax.random.randint(jax.random.fold_in(own_key, axis), (), 0, length) for axis, length in enumerate(entries.shape)]
    longest = entries.shape.index(max(entries.shape))
    beside = index_at[:longest] + [(index_at[longest] + 1) % entries.shape[longest]] + index_at[longest + 1:]
    return entries.at[tuple(index_at)].set(least).at[tuple(beside)].set(largest)


def block_levels(rng, extent, cuts, low, high):
    gain, own = 1.0, jax.random.fold_in(rng, 6)
    for dim, parts in cuts:
        steps = jnp.exp(jax.random.uniform(jax.random.fold_in(own, dim), (parts,), jnp.float32, low / len(cuts), high / len(cuts)))
        gain = gain * jnp.repeat(steps, extent[dim] // parts).reshape([-1 if axis == dim else 1 for axis in range(len(extent))])
    return gain


def scatter_about(stream_key, dims, scale, bound, cuts=(), held_as=jnp.bfloat16):
    values = scale * jax.random.normal(stream_key, dims, jnp.float32)
    if cuts:
        values = values * block_levels(stream_key, dims, cuts, -0.22, 0.18)
    return jnp.clip(values, -bound, bound).astype(held_as)


def setup_inputs(seed: int = 0) -> dict:
    seeds = jax.random.split(jax.random.key(seed), 5)
    ancestor_pivot = draw_ancestor_pivot(jax.random.fold_in(seeds[4], 71), 0)
    child_pivot = draw_child_pivot(jax.random.fold_in(seeds[4], 71), 0)
    child_panel = scatter_about(seeds[2], (LOC_A, N_ROW * BS, LOC_C, N_COL * BS), ANC ** -0.5, 0.09375, ((1, 4), (3, 8)), jnp.float32)
    block_pattern = with_ends((jax.random.randint(seeds[3], (ANB, SNB), 0, 2) < 1).astype(jnp.int32), jax.random.fold_in(seeds[3], 1), 0, 1)
    return {"ancestor_pivot": ancestor_pivot, "child_pivot": child_pivot, "child_panel": child_panel, "block_pattern": block_pattern}


def expand_pattern(block_pattern):
    unit = jnp.ones((1, BS, 1, BS), jnp.float32)
    return (block_pattern.astype(jnp.float32)[:, None, :, None] * unit).reshape(ANC, W)


def reference(ancestor_pivot, child_pivot, child_panel, block_pattern):
    ancestor = ancestor_pivot.reshape(ANC, ANC)
    child = child_pivot.reshape(W, W)
    masked = child_panel.reshape(ANC, W) * expand_pattern(block_pattern)
    ancestor_block = -jnp.dot(ancestor, masked, precision=lax.Precision.HIGHEST, preferred_element_type=jnp.float32)
    child_inverse = child - jnp.dot(masked.T, ancestor_block, precision=lax.Precision.HIGHEST, preferred_element_type=jnp.float32)
    return child_inverse.reshape(LOC_R, N_ROW * BS, LOC_C, N_COL * BS)
```

```python
import functools

import jax
import jax.numpy as jnp
from jax import lax
from jax.experimental import pallas as pl
from jax.experimental.pallas import tpu as pltpu
from jax.sharding import PartitionSpec as P

MESH = pl.DeviceIdType.MESH


def flip(index, mask):
    bit = 1
    while bit <= mask:
        if mask & bit:
            index = index + bit - 2 * bit * ((index // bit) % 2)
        bit *= 2
    return index


def halves_of(x):
    high = x.astype(jnp.bfloat16)
    return high, (x - high.astype(jnp.float32)).astype(jnp.bfloat16)


def dot3(a, b, dims):
    a_high, a_low = a
    b_high, b_low = b
    dot = functools.partial(
        lax.dot_general, dimension_numbers=(dims, ((), ())), preferred_element_type=jnp.float32
    )
    return dot(a_low, b_high) + dot(a_high, b_low) + dot(a_high, b_high)


def kernel(
    n_row, n_col, a_in, m_in, out, pieces, panel, slots, term, w_high, w_low, b_high, b_low,
    local_sem, col_send, col_recv, row_send, row_recv, sum_send, sum_recv,
):
    r = lax.axis_index("row")
    c = lax.axis_index("col")
    rows, cols = a_in.shape
    ratio = n_col // n_row
    half = rows // 2
    tile = min(rows, 256)
    strip = min(cols, 256)
    high_bits = [1 << i for i in range(1, n_col.bit_length() - 1)]
    orders = (high_bits + [1], high_bits[::-1] + [1])
    stages = len(orders[0])

    def col_copy(which, part, mask, bit):
        place = pieces.at[which, flip(c, mask), pl.ds(part * half, half)]
        return pltpu.make_async_remote_copy(
            src_ref=place,
            dst_ref=place,
            send_sem=col_send.at[which, part, mask ^ bit],
            recv_sem=col_recv.at[which, part, mask],
            device_id={"col": flip(c, bit)},
            device_id_type=MESH,
        )

    def col_send_piece(which, part, mask, bit):
        place = pieces.at[which, flip(c, mask), pl.ds(part * half, half)]
        pltpu.make_async_remote_copy(
            src_ref=place,
            dst_ref=place,
            send_sem=col_send.at[which, part, mask ^ bit],
            recv_sem=col_recv.at[which, part, mask ^ bit],
            device_id={"col": flip(c, bit)},
            device_id_type=MESH,
        ).start()

    def col_start(which):
        for s in range(stages):
            for part in range(2):
                col_send_piece(which, part, 0, orders[part][s])

    def col_stage(which, s):
        for part in range(2):
            order = orders[part]
            held = [0]
            for bit in order[:s]:
                held = held + [m ^ bit for m in held]
            for m in held:
                mask = m ^ order[s]
                col_copy(which, part, mask, order[s]).wait_recv()
                for bit in order[s + 1:]:
                    col_send_piece(which, part, mask, bit)

    def col_finish(which):
        for part in range(2):
            for mask in range(1, n_col):
                pltpu.make_async_remote_copy(
                    src_ref=pieces.at[which, c, pl.ds(part * half, half)],
                    dst_ref=pieces.at[which, c, pl.ds(part * half, half)],
                    send_sem=col_send.at[which, part, mask],
                    recv_sem=col_recv.at[which, part, mask],
                    device_id={"col": flip(c, 1)},
                    device_id_type=MESH,
                ).wait_send()

    def row_copy(d, block, step):
        return pltpu.make_async_remote_copy(
            src_ref=panel.at[block],
            dst_ref=panel.at[block],
            send_sem=row_send.at[d, step],
            recv_sem=row_recv.at[d, step],
            device_id={"row": (r + 1 - 2 * d + n_row) % n_row},
            device_id_type=MESH,
        )

    def sends(d, step):
        block = r - (step - 1) * (1 - 2 * d)
        there = r + 1 - 2 * d
        return block, (block >= 0) & (block < n_row) & (there >= 0) & (there < n_row)

    def receives(d, step):
        block = r - step * (1 - 2 * d)
        return block, (block >= 0) & (block < n_row)

    def row_start(step):
        for d in range(2):
            block, yes = sends(d, step)

            @pl.when(yes)
            def _():
                row_copy(d, block, step).start()

    def row_wait(step):
        for d in range(2):
            block, yes = receives(d, step)

            @pl.when(yes)
            def _():
                row_copy(d, block, step).wait_recv()

    def first_product(block):
        @pl.loop(0, ratio)
        def _(g):
            high, low = halves_of(panel[block, pl.ds(pl.multiple_of(g * cols, cols), cols), :])
            w_high[...] = high
            w_low[...] = low

            @pl.loop(0, rows // tile)
            def _(i):
                at = pl.ds(pl.multiple_of(i * tile, tile), tile)
                a = halves_of(pieces[0, block + g * n_row, at, :])
                out[at, :] += dot3(a, (w_high[...], w_low[...]), ((1,), (0,)))

    def first_products(step):
        @pl.loop(0, 2)
        def _(d):
            block, yes = receives(d, step)

            @pl.when(yes)
            def _():
                first_product(block)

    def second_product(block, g):
        @pl.loop(0, cols // strip)
        def _(i):
            at = pl.ds(pl.multiple_of(i * strip, strip), strip)
            m = halves_of(pieces[1, block + g * n_row, :, at])
            term[at, :] = dot3(m, (b_high[...], b_low[...]), ((0,), (0,)))

    def sum_copy(place, there_place, g, there):
        at = pl.ds(pl.multiple_of(g * cols, cols), cols)
        return pltpu.make_async_remote_copy(
            src_ref=slots.at[place, at],
            dst_ref=slots.at[there_place, at],
            send_sem=sum_send.at[place, g],
            recv_sem=sum_recv.at[there_place, g],
            device_id={"row": there},
            device_id_type=MESH,
        )

    copies = [
        pltpu.make_async_copy(a_in, pieces.at[0, c], local_sem.at[0]),
        pltpu.make_async_copy(m_in, panel.at[r], local_sem.at[1]),
        pltpu.make_async_copy(m_in, pieces.at[1, c], local_sem.at[2]),
    ]
    for copy in copies:
        copy.start()
    barrier = pltpu.get_barrier_semaphore()
    for bit in orders[0]:
        pl.semaphore_signal(barrier, inc=1, device_id={"col": flip(c, bit)}, device_id_type=MESH)
    for hop in (1, n_row - 1):
        pl.semaphore_signal(
            barrier, inc=1, device_id={"row": (r + hop) % n_row}, device_id_type=MESH
        )
    pl.semaphore_wait(barrier, stages + 2)
    for copy in copies:
        copy.wait()
    row_start(1)
    col_start(0)
    out[...] = jnp.zeros_like(out)
    col_stage(0, 0)
    row_wait(1)
    if n_row > 2:
        row_start(2)
    col_start(1)
    for s in range(1, stages):
        col_stage(0, s)
    first_product(r)
    for step in range(2, n_row):
        row_wait(step)
        if step + 1 < n_row:
            row_start(step + 1)
        if step == 2:
            col_stage(1, 0)
            first_products(1)
        if step + 1 == n_row:
            for s in range(1, stages - 1):
                col_stage(1, s)
        first_products(step)
    high, low = halves_of(out[...])
    b_high[...] = high
    b_low[...] = low
    col_stage(1, stages - 1)

    swap = (2 * r) // n_row

    def decode(index):
        u = index // (2 * ratio)
        g = (index // 2) % ratio
        d = (index + swap) % 2
        block = d * u + (1 - d) * (n_row - 1 - u)
        return g, d, block, (block - r) * (1 - 2 * d) > 0

    @pl.loop(0, (n_row - 1) * ratio * 2)
    def _(index):
        g, d, block, yes = decode(index)

        @pl.when(yes)
        def _():
            second_product(block, g)
            at = pl.ds(pl.multiple_of(g * cols, cols), cols)
            there = r + 1 - 2 * d
            fed = r * (1 - d) + (n_row - 1 - r) * d

            @pl.when(fed > 0)
            def _():
                sum_copy(block, block, g, there).wait_recv()
                slots[block, at, :] += term[...]

            @pl.when(fed <= 0)
            def _():
                slots[block, at, :] = term[...]

            last = jnp.where(block == there, d, 0)
            sum_copy(block, block + last * (n_row - block), g, there).start()

    beside = jnp.where(r > 0, r - 1, r + 1)

    @pl.loop(0, ratio)
    def _(g):
        at = pl.ds(pl.multiple_of(g * cols, cols), cols)
        second_product(r, g)
        out[at, :] = term[...]

        @pl.when(r > 0)
        def _():
            sum_copy(r, r, g, beside).wait_recv()
            out[at, :] += slots[r, at, :]

        @pl.when(r < n_row - 1)
        def _():
            sum_copy(r, n_row, g, beside).wait_recv()
            out[at, :] += slots[n_row, at, :]

    for which in range(2):
        col_finish(which)
    for step in range(1, n_row):
        for d in range(2):
            block, yes = sends(d, step)

            @pl.when(yes)
            def _():
                row_copy(d, block, step).wait_send()

    @pl.loop(0, (n_row - 1) * ratio * 2)
    def _(index):
        g, d, block, yes = decode(index)

        @pl.when(yes)
        def _():
            sum_copy(block, block, g, r + 1 - 2 * d).wait_send()


def local(n_row, n_col, ancestor_pivot, child_pivot, child_panel, block_pattern):
    blocks, size, col_blocks, width = child_panel.shape
    ratio = n_col // n_row
    rows, cols = blocks * size, col_blocks * width
    split = (col_blocks, ratio, size, cols)
    mask = block_pattern.reshape(blocks, n_row, col_blocks, n_col)
    mask = lax.dynamic_index_in_dim(mask, lax.axis_index("row"), 1, keepdims=False)
    mask = lax.dynamic_index_in_dim(mask, lax.axis_index("col"), 2, keepdims=False)
    masked = child_panel * mask.astype(jnp.float32)[:, None, :, None]

    def ordered(x):
        return jnp.transpose(x.reshape(split), (1, 0, 2, 3)).reshape(rows, cols)

    summed = pl.pallas_call(
        functools.partial(kernel, n_row, n_col),
        out_shape=jax.ShapeDtypeStruct((rows, cols), jnp.float32),
        in_specs=[pl.BlockSpec(memory_space=pl.ANY)] * 2,
        out_specs=pl.BlockSpec(memory_space=pltpu.VMEM),
        scratch_shapes=[
            pltpu.VMEM((2, n_col, rows, cols), jnp.float32),
            pltpu.VMEM((n_row, rows, cols), jnp.float32),
            pltpu.VMEM((n_row + 1, rows, cols), jnp.float32),
            pltpu.VMEM((cols, cols), jnp.float32),
            pltpu.VMEM((cols, cols), jnp.bfloat16),
            pltpu.VMEM((cols, cols), jnp.bfloat16),
            pltpu.VMEM((rows, cols), jnp.bfloat16),
            pltpu.VMEM((rows, cols), jnp.bfloat16),
            pltpu.SemaphoreType.DMA((3,)),
            pltpu.SemaphoreType.DMA((2, 2, n_col)),
            pltpu.SemaphoreType.DMA((2, 2, n_col)),
            pltpu.SemaphoreType.DMA((2, n_row)),
            pltpu.SemaphoreType.DMA((2, n_row)),
            pltpu.SemaphoreType.DMA((n_row + 1, ratio)),
            pltpu.SemaphoreType.DMA((n_row + 1, ratio)),
        ],
        compiler_params=pltpu.CompilerParams(
            collective_id=0, has_side_effects=True, vmem_limit_bytes=67043328
        ),
    )(ordered(ancestor_pivot), ordered(masked))
    back = jnp.transpose(summed.reshape(ratio, col_blocks, size, cols), (1, 0, 2, 3))
    return child_pivot + back.reshape(child_pivot.shape)


def solution(mesh):
    spec = P(None, "row", None, "col")
    return jax.shard_map(
        functools.partial(local, mesh.shape["row"], mesh.shape["col"]),
        mesh=mesh,
        in_specs=(spec, spec, spec, P()),
        out_specs=spec,
        check_vma=False,
    )
```

```python
import functools

import jax
import jax.numpy as jnp
from jax import lax
from jax.experimental import pallas as pl
from jax.experimental.pallas import tpu as pltpu
from jax.sharding import PartitionSpec as P

MESH = pl.DeviceIdType.MESH


def flip(index, mask):
    bit = 1
    while bit <= mask:
        if mask & bit:
            index = index + bit - 2 * bit * ((index // bit) % 2)
        bit *= 2
    return index


def halves_of(x):
    high = x.astype(jnp.bfloat16)
    return high, (x - high.astype(jnp.float32)).astype(jnp.bfloat16)


def dot3(a, b, dims):
    a_high, a_low = a
    b_high, b_low = b
    dot = functools.partial(
        lax.dot_general, dimension_numbers=(dims, ((), ())), preferred_element_type=jnp.float32
    )
    return dot(a_low, b_high) + dot(a_high, b_low) + dot(a_high, b_high)


def kernel(
    n_row, n_col, size, a_in, m_in, out, pieces, panel, slots, term, w_high, w_low, b_high, b_low,
    local_sem, col_send, col_recv, row_send, row_recv, sum_send, sum_recv,
):
    r = lax.axis_index("row")
    c = lax.axis_index("col")
    rows, cols = a_in.shape
    ratio = n_col // n_row
    blocks = rows // size
    half = rows // 2
    tile = min(rows, 256)
    strip = min(cols, 256)
    high_bits = [1 << i for i in range(1, n_col.bit_length() - 1)]
    orders = (high_bits + [1], high_bits[::-1] + [1])
    stages = len(orders[0])

    def col_copy(which, part, mask, bit):
        place = pieces.at[which, flip(c, mask), pl.ds(part * half, half)]
        return pltpu.make_async_remote_copy(
            src_ref=place,
            dst_ref=place,
            send_sem=col_send.at[which, part, mask ^ bit],
            recv_sem=col_recv.at[which, part, mask],
            device_id={"col": flip(c, bit)},
            device_id_type=MESH,
        )

    def col_send_piece(which, part, mask, bit):
        place = pieces.at[which, flip(c, mask), pl.ds(part * half, half)]
        pltpu.make_async_remote_copy(
            src_ref=place,
            dst_ref=place,
            send_sem=col_send.at[which, part, mask ^ bit],
            recv_sem=col_recv.at[which, part, mask ^ bit],
            device_id={"col": flip(c, bit)},
            device_id_type=MESH,
        ).start()

    def col_start(which):
        for s in range(stages):
            for part in range(2):
                col_send_piece(which, part, 0, orders[part][s])

    def col_stage(which, s):
        for part in range(2):
            order = orders[part]
            held = [0]
            for bit in order[:s]:
                held = held + [m ^ bit for m in held]
            for m in held:
                mask = m ^ order[s]
                col_copy(which, part, mask, order[s]).wait_recv()
                for bit in order[s + 1:]:
                    col_send_piece(which, part, mask, bit)

    def col_finish(which):
        for part in range(2):
            for mask in range(1, n_col):
                pltpu.make_async_remote_copy(
                    src_ref=pieces.at[which, c, pl.ds(part * half, half)],
                    dst_ref=pieces.at[which, c, pl.ds(part * half, half)],
                    send_sem=col_send.at[which, part, mask],
                    recv_sem=col_recv.at[which, part, mask],
                    device_id={"col": flip(c, 1)},
                    device_id_type=MESH,
                ).wait_send()

    def row_copy(d, block, step):
        return pltpu.make_async_remote_copy(
            src_ref=panel.at[block],
            dst_ref=panel.at[block],
            send_sem=row_send.at[d, step],
            recv_sem=row_recv.at[d, step],
            device_id={"row": (r + 1 - 2 * d + n_row) % n_row},
            device_id_type=MESH,
        )

    def sends(d, step):
        block = r - (step - 1) * (1 - 2 * d)
        there = r + 1 - 2 * d
        return block, (block >= 0) & (block < n_row) & (there >= 0) & (there < n_row)

    def receives(d, step):
        block = r - step * (1 - 2 * d)
        return block, (block >= 0) & (block < n_row)

    def row_start(step):
        for d in range(2):
            block, yes = sends(d, step)

            @pl.when(yes)
            def _():
                row_copy(d, block, step).start()

    def row_wait(step):
        for d in range(2):
            block, yes = receives(d, step)

            @pl.when(yes)
            def _():
                row_copy(d, block, step).wait_recv()

    def first_product(block):
        @pl.loop(0, ratio)
        def _(g):
            high, low = halves_of(panel[block, pl.ds(pl.multiple_of(g * cols, cols), cols), :])
            w_high[...] = high
            w_low[...] = low

            @pl.loop(0, rows // tile)
            def _(i):
                at = pl.ds(pl.multiple_of(i * tile, tile), tile)
                a = halves_of(pieces[0, block + g * n_row, at, :])
                out[at, :] += dot3(a, (w_high[...], w_low[...]), ((1,), (0,)))

    def first_products(step):
        @pl.loop(0, 2)
        def _(d):
            block, yes = receives(d, step)

            @pl.when(yes)
            def _():
                first_product(block)

    def second_product(block, g):
        @pl.loop(0, cols // strip)
        def _(i):
            at = pl.ds(pl.multiple_of(i * strip, strip), strip)
            m = halves_of(pieces[1, block + g * n_row, :, at])
            term[at, :] = dot3(m, (b_high[...], b_low[...]), ((0,), (0,)))

    def sum_copy(place, there_place, g, there):
        at = pl.ds(pl.multiple_of(g * cols, cols), cols)
        return pltpu.make_async_remote_copy(
            src_ref=slots.at[place, at],
            dst_ref=slots.at[there_place, at],
            send_sem=sum_send.at[place, g],
            recv_sem=sum_recv.at[there_place, g],
            device_id={"row": there},
            device_id_type=MESH,
        )

    copies = []
    for i in range(blocks):
        came = pl.ds(i * size, size)
        goes = pl.ds(((i % ratio) * (blocks // ratio) + i // ratio) * size, size)
        copies += [
            pltpu.make_async_copy(a_in.at[came], pieces.at[0, c, goes], local_sem.at[0, i]),
            pltpu.make_async_copy(m_in.at[came], panel.at[r, goes], local_sem.at[1, i]),
            pltpu.make_async_copy(m_in.at[came], pieces.at[1, c, goes], local_sem.at[2, i]),
        ]
    for copy in copies:
        copy.start()
    barrier = pltpu.get_barrier_semaphore()
    for bit in orders[0]:
        pl.semaphore_signal(barrier, inc=1, device_id={"col": flip(c, bit)}, device_id_type=MESH)
    for hop in (1, n_row - 1):
        pl.semaphore_signal(
            barrier, inc=1, device_id={"row": (r + hop) % n_row}, device_id_type=MESH
        )
    pl.semaphore_wait(barrier, stages + 2)
    for copy in copies:
        copy.wait()
    row_start(1)
    col_start(0)
    out[...] = jnp.zeros_like(out)
    col_stage(0, 0)
    row_wait(1)
    if n_row > 2:
        row_start(2)
    col_start(1)
    for s in range(1, stages):
        col_stage(0, s)
    first_product(r)
    for step in range(2, n_row):
        row_wait(step)
        if step + 1 < n_row:
            row_start(step + 1)
        if step == 2:
            col_stage(1, 0)
            first_products(1)
        if step + 1 == n_row:
            for s in range(1, stages - 1):
                col_stage(1, s)
        first_products(step)
    high, low = halves_of(out[...])
    b_high[...] = high
    b_low[...] = low
    col_stage(1, stages - 1)

    swap = (2 * r) // n_row

    def decode(index):
        u = index // (2 * ratio)
        g = (index // 2) % ratio
        d = (index + swap) % 2
        block = d * u + (1 - d) * (n_row - 1 - u)
        return g, d, block, (block - r) * (1 - 2 * d) > 0

    @pl.loop(0, (n_row - 1) * ratio * 2)
    def _(index):
        g, d, block, yes = decode(index)

        @pl.when(yes)
        def _():
            second_product(block, g)
            at = pl.ds(pl.multiple_of(g * cols, cols), cols)
            there = r + 1 - 2 * d
            fed = r * (1 - d) + (n_row - 1 - r) * d

            @pl.when(fed > 0)
            def _():
                sum_copy(block, block, g, there).wait_recv()
                slots[block, at, :] += term[...]

            @pl.when(fed <= 0)
            def _():
                slots[block, at, :] = term[...]

            last = jnp.where(block == there, d, 0)
            sum_copy(block, block + last * (n_row - block), g, there).start()

    beside = jnp.where(r > 0, r - 1, r + 1)

    @pl.loop(0, ratio)
    def _(g):
        at = pl.ds(pl.multiple_of(g * cols, cols), cols)
        second_product(r, g)

        @pl.when(r > 0)
        def _():
            sum_copy(r, r, g, beside).wait_recv()
            term[...] += slots[r, at, :]

        @pl.when(r < n_row - 1)
        def _():
            sum_copy(r, n_row, g, beside).wait_recv()
            term[...] += slots[n_row, at, :]

        for j in range(blocks // ratio):
            to = pl.ds(pl.multiple_of((ratio * j + g) * size, size), size)
            out[to, :] = term[pl.ds(j * size, size), :]

    for which in range(2):
        col_finish(which)
    for step in range(1, n_row):
        for d in range(2):
            block, yes = sends(d, step)

            @pl.when(yes)
            def _():
                row_copy(d, block, step).wait_send()

    @pl.loop(0, (n_row - 1) * ratio * 2)
    def _(index):
        g, d, block, yes = decode(index)

        @pl.when(yes)
        def _():
            sum_copy(block, block, g, r + 1 - 2 * d).wait_send()


def local(n_row, n_col, ancestor_pivot, child_pivot, child_panel, block_pattern):
    blocks, size, col_blocks, width = child_panel.shape
    ratio = n_col // n_row
    rows, cols = blocks * size, col_blocks * width
    mask = block_pattern.reshape(blocks, n_row, col_blocks, n_col)
    mask = lax.dynamic_index_in_dim(mask, lax.axis_index("row"), 1, keepdims=False)
    mask = lax.dynamic_index_in_dim(mask, lax.axis_index("col"), 2, keepdims=False)
    masked = child_panel * mask.astype(jnp.float32)[:, None, :, None]

    summed = pl.pallas_call(
        functools.partial(kernel, n_row, n_col, size),
        out_shape=jax.ShapeDtypeStruct((rows, cols), jnp.float32),
        in_specs=[pl.BlockSpec(memory_space=pl.ANY)] * 2,
        out_specs=pl.BlockSpec(memory_space=pltpu.VMEM),
        scratch_shapes=[
            pltpu.VMEM((2, n_col, rows, cols), jnp.float32),
            pltpu.VMEM((n_row, rows, cols), jnp.float32),
            pltpu.VMEM((n_row + 1, rows, cols), jnp.float32),
            pltpu.VMEM((cols, cols), jnp.float32),
            pltpu.VMEM((cols, cols), jnp.bfloat16),
            pltpu.VMEM((cols, cols), jnp.bfloat16),
            pltpu.VMEM((rows, cols), jnp.bfloat16),
            pltpu.VMEM((rows, cols), jnp.bfloat16),
            pltpu.SemaphoreType.DMA((3, blocks)),
            pltpu.SemaphoreType.DMA((2, 2, n_col)),
            pltpu.SemaphoreType.DMA((2, 2, n_col)),
            pltpu.SemaphoreType.DMA((2, n_row)),
            pltpu.SemaphoreType.DMA((2, n_row)),
            pltpu.SemaphoreType.DMA((n_row + 1, ratio)),
            pltpu.SemaphoreType.DMA((n_row + 1, ratio)),
        ],
        compiler_params=pltpu.CompilerParams(
            collective_id=0, has_side_effects=True, vmem_limit_bytes=67043328
        ),
    )(ancestor_pivot.reshape(rows, cols), masked.reshape(rows, cols))
    return child_pivot + summed.reshape(child_pivot.shape)


def solution(mesh):
    spec = P(None, "row", None, "col")
    return jax.shard_map(
        functools.partial(local, mesh.shape["row"], mesh.shape["col"]),
        mesh=mesh,
        in_specs=(spec, spec, spec, P()),
        out_specs=spec,
        check_vma=False,
    )
```
